32 devices in a mesh: vox: 8 (over y, x, core), fil: 4 (over z).
Axes of the slice: x: 2, y: 2, z: 4, core: 2. Of those that a mesh axis runs over, the one named last changes fastest.
Arguments:
- volume: bfloat16 [16, 16, 128, 256], P(None, 'vox', 'fil'), may hold values from -6 to 6
- fine_kernel: bfloat16 [16, 16, 3, 3, 3], replicated, may hold values from -0.3125 to 0.3125
- coarse_kernel: bfloat16 [64, 16, 3, 3, 3], replicated, may hold values from -0.3125 to 0.3125
- coarse_cot: bfloat16 [64, 8, 64, 128], P('fil', 'vox'), may hold values from -0.09375 to 0.09375
Outputs:
- coarse_out: bfloat16 [64, 8, 64, 128], P('fil', 'vox')
- grad_fine: float32 [16, 16, 3, 3, 3], replicated
- grad_coarse: float32 [64, 16, 3, 3, 3], replicated
The draws below stay inside these ranges and needn't reach their ends.
All inputs are finite; a program needn't handle non-finite values.
Results may differ from the reference program's by a relative error of at most 0.006.
Values may be sent and summed in bfloat16 or wider, within the bound.
A program may use at most 128 MiB of HBM per device.

```python
import jax
import jax.numpy as jnp
from jax import lax

C0 = 16
C1 = 64
NZ = 256
NX = 16
NY = 128


def level_of(rng, dims, cuts, least, high):
    factor_of = 1.0
    for axis_at, shards_of in cuts:
        draws = jax.random.uniform(jax.random.fold_in(jax.random.fold_in(rng, 6), axis_at), (shards_of,), jnp.float32, least / len(cuts), high / len(cuts))
        factor_of = factor_of * jnp.repeat(jnp.exp(draws), dims[axis_at] // shards_of).reshape((-1,) + (1,) * (len(dims) - 1 - axis_at))
    return factor_of


def gaussian(rng, dims, width, reach, cuts=(), kind=jnp.bfloat16):
    level = level_of(rng, dims, cuts, -0.22, 0.18) if cuts else 1.0
    result = jax.random.normal(rng, dims, jnp.float32) * width * level
    return jnp.minimum(jnp.maximum(result, -reach), reach).astype(kind)


def setup_inputs(seed: int = 0) -> dict:
    key_of = jax.random.split(jax.random.key(seed), 5)
    volume = gaussian(key_of[0], (C0, NX, NY, NZ), 1.0, 6.0, ((1, 8), (2, 4)))
    fine_kernel = gaussian(key_of[1], (C0, C0, 3, 3, 3), (C0 * 27) ** -0.5, 0.3125)
    coarse_kernel = gaussian(key_of[2], (C1, C0, 3, 3, 3), (C0 * 27) ** -0.5, 0.3125)
    coarse_cot = gaussian(key_of[3], (C1, NX // 2, NY // 2, NZ // 2), (4.0 * (8.0 / (NX * NY * NZ)) ** 0.5), 0.09375, ((0, 4), (1, 8)))
    return dict(volume=volume, fine_kernel=fine_kernel, coarse_kernel=coarse_kernel, coarse_cot=coarse_cot)


def conv_same(field, kernel):
    out = lax.conv_general_dilated(field.astype(jnp.float32)[None], kernel.astype(jnp.float32), (1, 1, 1), [(1, 1), (1, 1), (1, 1)], dimension_numbers=('NCDHW', 'OIDHW', 'NCDHW'), precision=lax.Precision.HIGHEST, preferred_element_type=jnp.float32)
    return out[0]

def kernel_grad(padded, cotangent):
    outs_count = cotangent.shape[0]
    ins_count = padded.shape[0]
    spans = cotangent.shape[1:]
    flat_cot = cotangent.astype(jnp.float32).reshape(outs_count, -1)
    pieces = []
    for first in range(3):
        for second in range(3):
            for third in range(3):
                window = lax.slice(padded, (0, first, second, third), (ins_count, first + spans[0], second + spans[1], third + spans[2]))
                flat_win = window.astype(jnp.float32).reshape(ins_count, -1)
                pieces.append(lax.dot_general(flat_cot, flat_win, (((1,), (1,)), ((), ())), precision=lax.Precision.HIGHEST, preferred_element_type=jnp.float32))
    stacked = jnp.stack(pieces, 2)
    return stacked.reshape(outs_count, ins_count, 3, 3, 3)

def pool_cubes(field):
    shape = field.shape
    return field.reshape(shape[0], shape[1] // 2, 2, shape[2] // 2, 2, shape[3] // 2, 2).mean(axis=(2, 4, 6))

def upsample(field):
    shape = field.shape
    wide = jnp.broadcast_to(field[:, :, None, :, None, :, None], (shape[0], shape[1], 2, shape[2], 2, shape[3], 2))
    return wide.reshape(shape[0], shape[1] * 2, shape[2] * 2, shape[3] * 2)

def reference(volume, fine_kernel, coarse_kernel, coarse_cot):
    preact = conv_same(volume, fine_kernel)
    pooled = pool_cubes(jnp.maximum(preact, 0.0)).astype(jnp.bfloat16)
    coarse_out = conv_same(pooled, coarse_kernel).astype(jnp.bfloat16)
    pooled_framed = jnp.pad(pooled, ((0, 0), (1, 1), (1, 1), (1, 1)))
    grad_coarse = kernel_grad(pooled_framed, coarse_cot)
    flipped = coarse_kernel[:, :, ::-1, ::-1, ::-1].transpose(1, 0, 2, 3, 4)
    returned = conv_same(coarse_cot, flipped)
    fine_cot = jnp.where(preact > 0, upsample(returned) * 0.125, 0.0).astype(jnp.bfloat16)
    volume_framed = jnp.pad(volume, ((0, 0), (1, 1), (1, 1), (1, 1)))
    grad_fine = kernel_grad(volume_framed, fine_cot)
    return (coarse_out, grad_fine, grad_coarse)
```

```python
import functools

import jax
import jax.numpy as jnp
from jax import lax
from jax.experimental import pallas as pl
from jax.experimental.pallas import tpu as pltpu

F32 = jnp.float32
BF16 = jnp.bfloat16
MESH = pl.DeviceIdType.MESH
SIDES = [(dv, df) for dv in (-1, 0, 1) for df in (-1, 0, 1) if (dv, df) != (0, 0)]


def dot(a, b):
    return jnp.dot(a, b, preferred_element_type=F32)


def dot_t(a, b):
    return lax.dot_general(a, b, (((1,), (1,)), ((), ())), preferred_element_type=F32)


def place():
    return lax.axis_index("vox"), lax.axis_index("fil")


def inside(v, f, dv, df, V, F):
    ok = None
    for at, step, size in ((v, dv, V), (f, df, F)):
        if step:
            here = (at + step >= 0) & (at + step < size)
            ok = here if ok is None else ok & here
    return ok


def remote(src, dst, send, recv, v, f):
    return pltpu.make_async_remote_copy(
        src_ref=src,
        dst_ref=dst,
        send_sem=send,
        recv_sem=recv,
        device_id={"vox": v, "fil": f},
        device_id_type=MESH,
    )


def signal(v, f):
    pl.semaphore_signal(
        pltpu.get_barrier_semaphore(), inc=1, device_id={"vox": v, "fil": f}, device_id_type=MESH
    )


def halo_views(dv, df, src, dst, planes, rows):
    sp = {1: pl.ds(planes - 1, 1), 0: pl.ds(0, planes), -1: pl.ds(0, 1)}[dv]
    dp = {1: pl.ds(0, 1), 0: pl.ds(1, planes), -1: pl.ds(planes + 1, 1)}[dv]
    sr = {1: pl.ds(rows - 1, 1), 0: pl.ds(0, rows), -1: pl.ds(0, 1)}[df]
    dr = {1: pl.ds(0, 1), 0: pl.ds(1, rows), -1: pl.ds(rows + 1, 1)}[df]
    return src.at[sp, sr], dst.at[dp, dr]


def halo_start(src, dst, sends, recvs, v, f, V, F):
    planes, rows = src.shape[:2]
    for n, (dv, df) in enumerate(SIDES):
        a, b = halo_views(dv, df, src, dst, planes, rows)

        @pl.when(inside(v, f, dv, df, V, F))
        def _():
            remote(a, b, sends.at[n], recvs.at[n], v + dv, f + df).start()

        @pl.when(jnp.logical_not(inside(v, f, -dv, -df, V, F)))
        def _():
            b[...] = jnp.zeros(b.shape, b.dtype)


def halo_wait(src, dst, sends, recvs, v, f, V, F):
    planes, rows = src.shape[:2]
    for n, (dv, df) in enumerate(SIDES):
        a, b = halo_views(dv, df, src, dst, planes, rows)

        @pl.when(inside(v, f, dv, df, V, F))
        def _():
            remote(a, b, sends.at[n], recvs.at[n], v + dv, f + df).wait_send()

        @pl.when(inside(v, f, -dv, -df, V, F))
        def _():
            remote(a, b, sends.at[n], recvs.at[n], v - dv, f - df).wait_recv()


def greet_sides(v, f, V, F):
    count = 0
    for dv, df in SIDES:
        ok = inside(v, f, dv, df, V, F)

        @pl.when(ok)
        def _():
            signal(v + dv, f + df)

        count = count + ok.astype(jnp.int32)
    return count


def inputs_kernel(V, F, vol, cot, vpad, cpad, vs, vr, cs, cr, ps, pr, ls):
    v, f = place()
    rows = cpad.shape[2]
    step = rows - 2
    count = greet_sides(v, f, V, F)
    for d in range(1, F):
        far = lax.rem(f + d, F)
        near = (far - f == 1) | (far - f == -1)

        @pl.when(jnp.logical_not(near))
        def _():
            signal(v, far)

        count = count + 1 - near.astype(jnp.int32)
    pl.semaphore_wait(pltpu.get_barrier_semaphore(), count)
    halo_start(vol, vpad, vs, vr, v, f, V, F)
    own = pltpu.make_async_copy(vol, vpad.at[pl.ds(1, vol.shape[0]), pl.ds(1, vol.shape[1])], ls.at[0])
    own.start()
    mine = pltpu.make_async_copy(cot.at[pl.ds(f * step, rows)], cpad.at[1, f], ls.at[1])
    mine.start()
    copies = []
    for d in range(1, F):
        far = lax.rem(f + d, F)
        copies.append(
            remote(cot.at[pl.ds(far * step, rows)], cpad.at[1, f], cs.at[d], cr.at[d], v, far)
        )
        copies[-1].start()
    for side in (0, 1):
        edge = v == (0 if side == 0 else V - 1)

        @pl.when(edge)
        def _():
            cpad[2 * side] = jnp.zeros(cpad.shape[1:], cpad.dtype)

    mine.wait()
    for c in copies:
        c.wait_recv()
    for side, dv in ((0, 1), (1, -1)):

        @pl.when(inside(v, f, dv, 0, V, F))
        def _():
            remote(cpad.at[1], cpad.at[2 * side], ps.at[side], pr.at[side], v + dv, f).start()

    own.wait()
    halo_wait(vol, vpad, vs, vr, v, f, V, F)
    for c in copies:
        c.wait_send()
    for side, dv in ((0, 1), (1, -1)):
        c = remote(cpad.at[1], cpad.at[2 * side], ps.at[side], pr.at[side], v, f)

        @pl.when(inside(v, f, dv, 0, V, F))
        def _():
            c.wait_send()

        @pl.when(inside(v, f, -dv, 0, V, F))
        def _():
            c.wait_recv()


def pooled_kernel(V, F, pooled, ppad, sends, recvs, ls):
    v, f = place()
    count = greet_sides(v, f, V, F)
    pl.semaphore_wait(pltpu.get_barrier_semaphore(), count)
    halo_start(pooled, ppad, sends, recvs, v, f, V, F)
    own = pltpu.make_async_copy(pooled, ppad.at[pl.ds(1, 1), pl.ds(1, pooled.shape[1])], ls)
    own.start()
    own.wait()
    halo_wait(pooled, ppad, sends, recvs, v, f, V, F)


def outputs_kernel(V, F, co, g, out, total, slots, red, os, orr, ss, rs, ls):
    v, f = place()
    n = V * F
    me = v * F + f
    rows = co.shape[1]
    chunk = red.shape[0]

    def peer_of(d):
        p = lax.rem(me + d, n)
        return p, p // F, lax.rem(p, F)

    def greet(d, c):
        _, pv, pf = peer_of(d)
        signal(pv, pf)
        return c

    lax.fori_loop(1, n, greet, 0)
    pl.semaphore_wait(pltpu.get_barrier_semaphore(), n - 1)

    def scatter(d, c):
        p, pv, pf = peer_of(d)
        remote(g.at[pl.ds(pl.multiple_of(p * chunk, chunk), chunk)], slots.at[d - 1], ss.at[0], rs.at[0], pv, pf).start()
        return c

    lax.fori_loop(1, n, scatter, 0)
    mine = pltpu.make_async_copy(co.at[f], out.at[pl.ds(f * rows, rows)], ls)
    mine.start()
    copies = []
    for d in range(1, F):
        far = lax.rem(f + d, F)
        copies.append(remote(co.at[far], out.at[pl.ds(f * rows, rows)], os.at[d], orr.at[d], v, far))
        copies[-1].start()
    pltpu.make_async_copy(slots, slots, rs.at[0]).wait()
    here = pl.ds(pl.multiple_of(me * chunk, chunk), chunk)
    red[...] = g[here] + jnp.sum(slots[...], axis=0)
    total[here] = red[...]

    def gather(d, c):
        _, pv, pf = peer_of(d)
        remote(red, total.at[here], ss.at[1], rs.at[1], pv, pf).start()
        return c

    lax.fori_loop(1, n, gather, 0)
    mine.wait()
    for c in copies:
        c.wait()
    pltpu.make_async_copy(slots, slots, ss.at[0]).wait()
    pltpu.make_async_copy(slots, slots, rs.at[1]).wait()
    pltpu.make_async_copy(slots, slots, ss.at[1]).wait()


def fine_kernel_body(vpad, w, sh, mask, pooled):
    planes, rows, chans, cols = vpad.shape
    half = cols // 2
    x = lax.broadcasted_iota(jnp.int32, (cols, cols), 0)
    y = lax.broadcasted_iota(jnp.int32, (cols, cols), 1)
    home = jnp.where(y < half, 2 * y, 2 * (y - half) + 1)
    for s in range(3):
        pick = jnp.where(x == home + (s - 1), 1.0, 0.0).astype(BF16)
        for p in range(planes):
            flat = vpad[p].reshape(rows * chans, cols)
            sh[s, p] = dot(flat, pick).astype(BF16).reshape(rows, chans, cols)

    def body(r, c):
        d = sh[:, :, pl.ds(2 * r, 4)].reshape(w.shape[1], cols)
        pre = dot(w[...], d)
        mask[r] = jnp.where(pre > 0, 1.0, 0.0).astype(BF16)
        act = jnp.maximum(pre, 0.0)
        s4 = act[0:chans] + act[chans : 2 * chans] + act[2 * chans : 3 * chans] + act[3 * chans :]
        pooled[0, r] = ((s4[:, :half] + s4[:, half:]) * 0.125).astype(BF16)
        return c

    lax.fori_loop(0, pooled.shape[1], body, 0, unroll=4)


def coarse_kernel_body(ppad, cpad, ck, rk, mask, sh, co, g, psh, csh, gc, gf):
    chans, half = ppad.shape[2:]
    F, rows2 = cpad.shape[1:3]
    filters = cpad.shape[3]
    rows = rows2 - 2
    x = lax.broadcasted_iota(jnp.int32, (half, half), 0)
    y = lax.broadcasted_iota(jnp.int32, (half, half), 1)
    for s in range(3):
        pick = jnp.where(x == y + (s - 1), 1.0, 0.0).astype(BF16)
        for p in range(3):
            a = ppad[p]
            if s != 1:
                a = dot(a.reshape(-1, half), pick).astype(BF16).reshape(a.shape)
            psh[s, p] = a
            for k in range(F):
                b = cpad[p, k]
                if s != 1:
                    b = dot(b.reshape(-1, half), pick).astype(BF16).reshape(b.shape)
                csh[s, p, :, pl.ds(k * filters, filters)] = b
    gc[...] = jnp.zeros(gc.shape, F32)
    gf[...] = jnp.zeros(gf.shape, F32)

    def body(r, c):
        dp = psh[:, :, pl.ds(r, 3)].reshape(ck.shape[1], half)
        o = dot(ck[...], dp).astype(BF16)
        co[:, r] = o.reshape(F, filters, half)
        gc[...] += dot_t(dp, csh[1, 1, r + 1])
        dc = csh[:, :, pl.ds(r, 3)].reshape(rk.shape[1], half)
        ret = (dot(rk[...], dc) * 0.125).astype(BF16)
        wide = jnp.concatenate([ret, ret], axis=1)
        fc = jnp.concatenate([wide] * 4, axis=0) * mask[r]
        d = sh[:, :, pl.ds(2 * r, 4)].reshape(48 * chans, 2 * half)
        gf[...] += dot_t(d, fc)
        return c

    lax.fori_loop(0, rows, body, 0, unroll=2)
    full = gf[...].reshape(3, 4, 4, chans, 4 * chans)
    fine = None
    for p in range(2):
        for r in range(2):
            q = (2 * p + r) * chans
            part = full[:, p : p + 3, r : r + 3].reshape(27 * chans, 4 * chans)[:, q : q + chans]
            fine = part if fine is None else fine + part
    n = gc.shape[0]
    g[...] = jnp.zeros(g.shape, F32)
    g[0:n, 0 : gc.shape[1]] = gc[...]
    g[0:n, gc.shape[1] : gc.shape[1] + chans] = fine


def local(V, F, volume, fine_kernel, coarse_kernel, coarse_cot):
    chans, planes, frows, cols = volume.shape
    filters, _, allrows, half = coarse_cot.shape
    rows = allrows // F
    outs = filters * F
    n = V * F
    taps = 27 * chans
    chunk = 8 * (-(-taps // (8 * n)))
    vmem = pl.BlockSpec(memory_space=pltpu.VMEM)
    dma = pltpu.SemaphoreType.DMA

    def call(body, ins, outputs, scratch, ident=None):
        extra = {} if ident is None else dict(collective_id=ident, has_side_effects=True)
        return pl.pallas_call(
            body,
            out_shape=[jax.ShapeDtypeStruct(s, t) for s, t in outputs],
            in_specs=[vmem] * ins,
            out_specs=[vmem] * len(outputs),
            scratch_shapes=scratch,
            compiler_params=pltpu.CompilerParams(vmem_limit_bytes=56 * 2**20, **extra),
        )

    vol_t = volume.transpose(1, 2, 0, 3)
    cot_t = jnp.pad(coarse_cot[:, 0].transpose(1, 0, 2), ((1, 1), (0, 0), (0, 0)))
    parts = []
    fk = fine_kernel.transpose(0, 4, 2, 3, 1)
    for p in range(2):
        for r in range(2):
            parts.append(jnp.pad(fk, ((0, 0), (0, 0), (p, 1 - p), (r, 1 - r), (0, 0))))
    w = jnp.stack(parts).reshape(4 * chans, 48 * chans)
    ck = coarse_kernel.transpose(0, 4, 2, 3, 1).reshape(outs, taps)
    rk = coarse_kernel[:, :, ::-1, ::-1, ::-1].transpose(1, 4, 2, 3, 0).reshape(chans, 27 * outs)

    vpad, cpad = call(
        functools.partial(inputs_kernel, V, F),
        2,
        [((planes + 2, frows + 2, chans, cols), BF16), ((3, F, rows + 2, filters, half), BF16)],
        [dma((8,)), dma((8,)), dma((F,)), dma((F,)), dma((2,)), dma((2,)), dma((2,))],
        0,
    )(vol_t, cot_t)
    sh, mask, pooled = call(
        fine_kernel_body,
        2,
        [
            ((3, planes + 2, frows + 2, chans, cols), BF16),
            ((rows, 4 * chans, cols), BF16),
            ((1, rows, chans, half), BF16),
        ],
        [],
    )(vpad, w)
    (ppad,) = call(
        functools.partial(pooled_kernel, V, F),
        1,
        [((3, rows + 2, chans, half), BF16)],
        [dma((8,)), dma((8,)), dma],
        1,
    )(pooled)
    co, g = call(
        coarse_kernel_body,
        6,
        [((F, rows, filters, half), BF16), ((n * chunk, 128), F32)],
        [
            pltpu.VMEM((3, 3, rows + 2, chans, half), BF16),
            pltpu.VMEM((3, 3, rows + 2, outs, half), BF16),
            pltpu.VMEM((taps, outs), F32),
            pltpu.VMEM((48 * chans, 4 * chans), F32),
        ],
    )(ppad, cpad, ck, rk, mask, sh)
    out, total = call(
        functools.partial(outputs_kernel, V, F),
        2,
        [((allrows, filters, half), BF16), ((n * chunk, 128), F32)],
        [
            pltpu.VMEM((n - 1, chunk, 128), F32),
            pltpu.VMEM((chunk, 128), F32),
            dma((F,)),
            dma((F,)),
            dma((2,)),
            dma((2,)),
            dma,
        ],
        2,
    )(co, g)
    coarse_out = out.transpose(1, 0, 2)[:, None]
    whole = total[:taps].reshape(3, 3, 3, chans, 128).transpose(4, 3, 1, 2, 0)
    return coarse_out, whole[outs : outs + chans], whole[:outs]


def solution(mesh):
    from jax.sharding import PartitionSpec as P

    in_specs = (P(None, "vox", "fil", None), P(), P(), P("fil", "vox", None, None))
    out_specs = (P("fil", "vox", None, None), P(), P())
    body = functools.partial(local, mesh.shape["vox"], mesh.shape["fil"])
    return jax.shard_map(body, mesh=mesh, in_specs=in_specs, out_specs=out_specs, check_vma=False)
```

```python
import functools

import jax
import jax.numpy as jnp
from jax import lax
from jax.experimental import pallas as pl
from jax.experimental.pallas import tpu as pltpu

F32 = jnp.float32
BF16 = jnp.bfloat16
MESH = pl.DeviceIdType.MESH
SIDES = [(dv, df) for dv in (-1, 0, 1) for df in (-1, 0, 1) if (dv, df) != (0, 0)]


def dot(a, b):
    return jnp.dot(a, b, preferred_element_type=F32)


def dot_t(a, b):
    return lax.dot_general(a, b, (((1,), (1,)), ((), ())), preferred_element_type=F32)


def place():
    return lax.axis_index("vox"), lax.axis_index("fil")


def inside(v, f, dv, df, V, F):
    ok = None
    for at, step, size in ((v, dv, V), (f, df, F)):
        if step:
            here = (at + step >= 0) & (at + step < size)
            ok = here if ok is None else ok & here
    return ok


def remote(src, dst, send, recv, v, f):
    return pltpu.make_async_remote_copy(
        src_ref=src,
        dst_ref=dst,
        send_sem=send,
        recv_sem=recv,
        device_id={"vox": v, "fil": f},
        device_id_type=MESH,
    )


def signal(v, f):
    pl.semaphore_signal(
        pltpu.get_barrier_semaphore(), inc=1, device_id={"vox": v, "fil": f}, device_id_type=MESH
    )


def halo_views(dv, df, src, dst, planes, rows):
    sp = {1: pl.ds(planes - 1, 1), 0: pl.ds(0, planes), -1: pl.ds(0, 1)}[dv]
    dp = {1: pl.ds(0, 1), 0: pl.ds(1, planes), -1: pl.ds(planes + 1, 1)}[dv]
    sr = {1: pl.ds(rows - 1, 1), 0: pl.ds(0, rows), -1: pl.ds(0, 1)}[df]
    dr = {1: pl.ds(0, 1), 0: pl.ds(1, rows), -1: pl.ds(rows + 1, 1)}[df]
    return src.at[sp, sr], dst.at[dp, dr]


def halo_start(src, dst, sends, recvs, v, f, V, F):
    planes, rows = src.shape[:2]
    for n, (dv, df) in enumerate(SIDES):
        a, b = halo_views(dv, df, src, dst, planes, rows)

        @pl.when(inside(v, f, dv, df, V, F))
        def _():
            remote(a, b, sends.at[n], recvs.at[n], v + dv, f + df).start()

        @pl.when(jnp.logical_not(inside(v, f, -dv, -df, V, F)))
        def _():
            b[...] = jnp.zeros(b.shape, b.dtype)


def halo_wait(src, dst, sends, recvs, v, f, V, F):
    planes, rows = src.shape[:2]
    for n, (dv, df) in enumerate(SIDES):
        a, b = halo_views(dv, df, src, dst, planes, rows)

        @pl.when(inside(v, f, dv, df, V, F))
        def _():
            remote(a, b, sends.at[n], recvs.at[n], v + dv, f + df).wait_send()

        @pl.when(inside(v, f, -dv, -df, V, F))
        def _():
            remote(a, b, sends.at[n], recvs.at[n], v - dv, f - df).wait_recv()


def greet_sides(v, f, V, F):
    count = 0
    for dv, df in SIDES:
        ok = inside(v, f, dv, df, V, F)

        @pl.when(ok)
        def _():
            signal(v + dv, f + df)

        count = count + ok.astype(jnp.int32)
    return count


def whole_kernel(
    V, F,
    vol, cot, w, ck, rk,
    out, total,
    vpad, cpad, sh, mask, ppad, psh, csh, gc, gf, co, g, slots, red,
    vs, vr, cs, cr, ts, tr, ps, pr, os, orr, ss, rs, ls,
):
    v, f = place()
    n = V * F
    me = v * F + f
    planes, frows, chans, cols = vol.shape
    half = cols // 2
    rows = frows // 2
    filters = co.shape[2]
    outs = filters * F
    chunk = red.shape[0]

    def peer_of(d):
        p = lax.rem(me + d, n)
        return p, p // F, lax.rem(p, F)

    def greet(d, c):
        _, pv, pf = peer_of(d)
        signal(pv, pf)
        return c

    lax.fori_loop(1, n, greet, 0)

    x = lax.broadcasted_iota(jnp.int32, (cols, cols), 0)
    y = lax.broadcasted_iota(jnp.int32, (cols, cols), 1)
    home = jnp.where(y < half, 2 * y, 2 * (y - half) + 1)
    x1 = lax.broadcasted_iota(jnp.int32, (half, half), 0)
    y1 = lax.broadcasted_iota(jnp.int32, (half, half), 1)

    def pick2(s):
        return jnp.where(x == home + (s - 1), 1.0, 0.0).astype(BF16)

    def pick1(s):
        return jnp.where(x1 == y1 + (s - 1), 1.0, 0.0).astype(BF16)

    def shift_fine(p, r, block):
        flat = block.reshape(-1, cols)
        for s in range(3):
            sh[s, p, r] = dot(flat, pick2(s)).astype(BF16).reshape(block.shape)

    for p in range(planes):
        shift_fine(1 + p, pl.ds(1, frows), vol[p])
    gc[...] = jnp.zeros(gc.shape, F32)
    gf[...] = jnp.zeros(gf.shape, F32)
    g[...] = jnp.zeros(g.shape, g.dtype)

    pl.semaphore_wait(pltpu.get_barrier_semaphore(), n - 1)

    halo_start(vol, vpad, vs, vr, v, f, V, F)
    copies = []
    for d in range(1, F):
        far = lax.rem(f + d, F)
        copies.append(
            remote(cot.at[pl.ds(far * rows, rows + 2)], cpad.at[1, f], cs.at[d], cr.at[d], v, far)
        )
        copies[-1].start()
    mine = pltpu.make_async_copy(cot.at[pl.ds(f * rows, rows + 2)], cpad.at[1, f], ls.at[0])
    mine.start()
    for side in (0, 1):

        @pl.when(v == (0 if side == 0 else V - 1))
        def _():
            cpad[2 * side] = jnp.zeros(cpad.shape[1:], cpad.dtype)

    halo_wait(vol, vpad, vs, vr, v, f, V, F)
    for p in (0, planes + 1):
        shift_fine(p, pl.ds(0, frows + 2), vpad[p])
    for r in (0, frows + 1):
        shift_fine(pl.ds(1, planes), r, vpad[pl.ds(1, planes), r])

    def fine(r, c):
        d = sh[:, :, pl.ds(2 * r, 4)].reshape(w.shape[1], cols)
        pre = dot(w[...], d)
        mask[r] = jnp.where(pre > 0, 1.0, 0.0).astype(BF16)
        act = jnp.maximum(pre, 0.0)
        s4 = act[0:chans] + act[chans : 2 * chans] + act[2 * chans : 3 * chans] + act[3 * chans :]
        ppad[1, 1 + r] = ((s4[:, :half] + s4[:, half:]) * 0.125).astype(BF16)
        return c

    lax.fori_loop(0, rows // 2, fine, 0, unroll=4)
    mine.wait()
    for c in copies:
        c.wait_recv()
    for side, dv in ((0, 1), (1, -1)):

        @pl.when(inside(v, f, dv, 0, V, F))
        def _():
            remote(cpad.at[1], cpad.at[2 * side], ts.at[side], tr.at[side], v + dv, f).start()

    lax.fori_loop(rows // 2, rows, fine, 0, unroll=4)

    own = ppad.at[pl.ds(1, 1), pl.ds(1, rows)]
    halo_start(own, ppad, ps, pr, v, f, V, F)

    def shift_cot(p):
        for k in range(F):
            b = cpad[p, k]
            for s in range(3):
                m = b
                if s != 1:
                    m = dot(b.reshape(-1, half), pick1(s)).astype(BF16).reshape(b.shape)
                csh[s, p, :, pl.ds(k * filters, filters)] = m

    shift_cot(1)
    for c in copies:
        c.wait_send()
    for side, dv in ((0, 1), (1, -1)):
        c = remote(cpad.at[1], cpad.at[2 * side], ts.at[side], tr.at[side], v, f)

        @pl.when(inside(v, f, dv, 0, V, F))
        def _():
            c.wait_send()

        @pl.when(inside(v, f, -dv, 0, V, F))
        def _():
            c.wait_recv()

    shift_cot(0)
    shift_cot(2)

    def pair(ref, r, size):
        one = ref[:, :, pl.ds(r, 3)].reshape(size, half)
        two = ref[:, :, pl.ds(r + 1, 3)].reshape(size, half)
        return jnp.concatenate([one, two], axis=1)

    def back(t, c):
        r = 2 * t
        ret = (dot(rk[...], pair(csh, r, rk.shape[1])) * 0.125).astype(BF16)
        for k in range(2):
            part = ret[:, k * half : (k + 1) * half]
            wide = jnp.concatenate([part, part], axis=1)
            fc = jnp.concatenate([wide] * 4, axis=0) * mask[r + k]
            d = sh[:, :, pl.ds(2 * (r + k), 4)].reshape(48 * chans, cols)
            gf[...] += dot_t(d, fc)
        return c

    lax.fori_loop(0, rows // 2, back, 0)
    full = gf[...].reshape(3, 4, 4, chans, 4 * chans)
    sums = None
    for p in range(2):
        for r in range(2):
            q = (2 * p + r) * chans
            part = full[:, p : p + 3, r : r + 3].reshape(27 * chans, 4 * chans)[:, q : q + chans]
            sums = part if sums is None else sums + part
    taps = gc.shape[0]
    g[0:taps, outs : outs + chans] = sums.astype(g.dtype)

    halo_wait(own, ppad, ps, pr, v, f, V, F)
    for p in range(3):
        a = ppad[p]
        for s in range(3):
            m = a
            if s != 1:
                m = dot(a.reshape(-1, half), pick1(s)).astype(BF16).reshape(a.shape)
            psh[s, p] = m

    def coarse_grad(t, c):
        r = 2 * t
        both = jnp.concatenate([csh[1, 1, r + 1], csh[1, 1, r + 2]], axis=1)
        gc[...] += dot_t(pair(psh, r, taps), both)
        return c

    lax.fori_loop(0, rows // 2, coarse_grad, 0, unroll=2)
    g[0:taps, 0:outs] = gc[...].astype(g.dtype)

    def scatter(d, c):
        p, pv, pf = peer_of(d)
        src = g.at[pl.ds(pl.multiple_of(p * chunk, chunk), chunk)]
        remote(src, slots.at[d - 1], ss.at[0], rs.at[0], pv, pf).start()
        return c

    lax.fori_loop(1, n, scatter, 0)

    def coarse(t, c):
        r = 2 * t
        o = dot(ck[...], pair(psh, r, taps)).astype(BF16)
        co[:, r] = o[:, :half].reshape(F, filters, half)
        co[:, r + 1] = o[:, half:].reshape(F, filters, half)
        return c

    lax.fori_loop(0, rows // 2, coarse, 0, unroll=2)
    mine = pltpu.make_async_copy(co.at[f], out.at[pl.ds(f * rows, rows)], ls.at[1])
    mine.start()
    copies = []
    for d in range(1, F):
        far = lax.rem(f + d, F)
        copies.append(remote(co.at[far], out.at[pl.ds(f * rows, rows)], os.at[d], orr.at[d], v, far))
        copies[-1].start()
    pltpu.make_async_copy(slots, slots, rs.at[0]).wait()
    here = pl.ds(pl.multiple_of(me * chunk, chunk), chunk)
    red[...] = (g[here].astype(F32) + jnp.sum(slots[...].astype(F32), axis=0)).astype(red.dtype)
    total[here] = red[...]

    def gather(d, c):
        _, pv, pf = peer_of(d)
        remote(red, total.at[here], ss.at[1], rs.at[1], pv, pf).start()
        return c

    lax.fori_loop(1, n, gather, 0)
    mine.wait()
    for c in copies:
        c.wait()
    pltpu.make_async_copy(slots, slots, ss.at[0]).wait()
    pltpu.make_async_copy(slots, slots, rs.at[1]).wait()
    pltpu.make_async_copy(slots, slots, ss.at[1]).wait()


def local(V, F, volume, fine_kernel, coarse_kernel, coarse_cot):
    chans, planes, frows, cols = volume.shape
    filters, _, allrows, half = coarse_cot.shape
    rows = allrows // F
    outs = filters * F
    n = V * F
    taps = 27 * chans
    chunk = 16 * (-(-taps // (16 * n)))
    vmem = pl.BlockSpec(memory_space=pltpu.VMEM)
    dma = pltpu.SemaphoreType.DMA

    def call(body, ins, outputs, scratch, ident=None):
        extra = {} if ident is None else dict(collective_id=ident, has_side_effects=True)
        return pl.pallas_call(
            body,
            out_shape=[jax.ShapeDtypeStruct(s, t) for s, t in outputs],
            in_specs=[vmem] * ins,
            out_specs=[vmem] * len(outputs),
            scratch_shapes=scratch,
            compiler_params=pltpu.CompilerParams(vmem_limit_bytes=56 * 2**20, **extra),
        )

    vol_t = volume.transpose(1, 2, 0, 3)
    cot_t = jnp.pad(coarse_cot[:, 0].transpose(1, 0, 2), ((1, 1), (0, 0), (0, 0)))
    parts = []
    fk = fine_kernel.transpose(0, 4, 2, 3, 1)
    for p in range(2):
        for r in range(2):
            parts.append(jnp.pad(fk, ((0, 0), (0, 0), (p, 1 - p), (r, 1 - r), (0, 0))))
    w = jnp.stack(parts).reshape(4 * chans, 48 * chans)
    ck = coarse_kernel.transpose(0, 4, 2, 3, 1).reshape(outs, taps)
    rk = coarse_kernel[:, :, ::-1, ::-1, ::-1].transpose(1, 4, 2, 3, 0).reshape(chans, 27 * outs)

    out, total = call(
        functools.partial(whole_kernel, V, F),
        5,
        [((allrows, filters, half), BF16), ((n * chunk, 128), BF16)],
        [
            pltpu.VMEM((planes + 2, frows + 2, chans, cols), BF16),
            pltpu.VMEM((3, F, rows + 2, filters, half), BF16),
            pltpu.VMEM((3, planes + 2, frows + 2, chans, cols), BF16),
            pltpu.VMEM((rows, 4 * chans, cols), BF16),
            pltpu.VMEM((3, rows + 2, chans, half), BF16),
            pltpu.VMEM((3, 3, rows + 2, chans, half), BF16),
            pltpu.VMEM((3, 3, rows + 2, outs, half), BF16),
            pltpu.VMEM((taps, outs), F32),
            pltpu.VMEM((48 * chans, 4 * chans), F32),
            pltpu.VMEM((F, rows, filters, half), BF16),
            pltpu.VMEM((n * chunk, 128), BF16),
            pltpu.VMEM((n - 1, chunk, 128), BF16),
            pltpu.VMEM((chunk, 128), BF16),
        ]
        + [dma((k,)) for k in (8, 8, F, F, 2, 2, 8, 8, F, F, 2, 2, 2)],
        0,
    )(vol_t, cot_t, w, ck, rk)
    coarse_out = out.transpose(1, 0, 2)[:, None]
    whole = total[:taps].astype(F32).reshape(3, 3, 3, chans, 128).transpose(4, 3, 1, 2, 0)
    return coarse_out, whole[outs : outs + chans], whole[:outs]


def solution(mesh):
    from jax.sharding import PartitionSpec as P

    in_specs = (P(None, "vox", "fil", None), P(), P(), P("fil", "vox", None, None))
    out_specs = (P("fil", "vox", None, None), P(), P())
    body = functools.partial(local, mesh.shape["vox"], mesh.shape["fil"])
    return jax.shard_map(body, mesh=mesh, in_specs=in_specs, out_specs=out_specs, check_vma=False)
```

```python
import functools

import jax
import jax.numpy as jnp
from jax import lax
from jax.experimental import pallas as pl
from jax.experimental.pallas import tpu as pltpu

F32 = jnp.float32
BF16 = jnp.bfloat16
MESH = pl.DeviceIdType.MESH
SIDES = [(dv, df) for dv in (-1, 0, 1) for df in (-1, 0, 1) if (dv, df) != (0, 0)]


def dot(a, b):
    return jnp.dot(a, b, preferred_element_type=F32)


def dot_t(a, b):
    return lax.dot_general(a, b, (((1,), (1,)), ((), ())), preferred_element_type=F32)


def place():
    return lax.axis_index("vox"), lax.axis_index("fil")


def inside(v, f, dv, df, V, F):
    ok = None
    for at, step, size in ((v, dv, V), (f, df, F)):
        if step:
            here = (at + step >= 0) & (at + step < size)
            ok = here if ok is None else ok & here
    return ok


def remote(src, dst, send, recv, v, f):
    return pltpu.make_async_remote_copy(
        src_ref=src,
        dst_ref=dst,
        send_sem=send,
        recv_sem=recv,
        device_id={"vox": v, "fil": f},
        device_id_type=MESH,
    )


def signal(v, f):
    pl.semaphore_signal(
        pltpu.get_barrier_semaphore(), inc=1, device_id={"vox": v, "fil": f}, device_id_type=MESH
    )


def halo_views(dv, df, src, dst, planes, rows):
    sp = {1: pl.ds(planes - 1, 1), 0: pl.ds(0, planes), -1: pl.ds(0, 1)}[dv]
    dp = {1: pl.ds(0, 1), 0: pl.ds(1, planes), -1: pl.ds(planes + 1, 1)}[dv]
    sr = {1: pl.ds(rows - 1, 1), 0: pl.ds(0, rows), -1: pl.ds(0, 1)}[df]
    dr = {1: pl.ds(0, 1), 0: pl.ds(1, rows), -1: pl.ds(rows + 1, 1)}[df]
    return src.at[sp, sr], dst.at[dp, dr]


def halo_start(src, dst, sends, recvs, v, f, V, F):
    planes, rows = src.shape[:2]
    for n, (dv, df) in enumerate(SIDES):
        a, b = halo_views(dv, df, src, dst, planes, rows)

        @pl.when(inside(v, f, dv, df, V, F))
        def _():
            remote(a, b, sends.at[n], recvs.at[n], v + dv, f + df).start()

        @pl.when(jnp.logical_not(inside(v, f, -dv, -df, V, F)))
        def _():
            b[...] = jnp.zeros(b.shape, b.dtype)


def halo_wait(src, dst, sends, recvs, v, f, V, F):
    planes, rows = src.shape[:2]
    for n, (dv, df) in enumerate(SIDES):
        a, b = halo_views(dv, df, src, dst, planes, rows)

        @pl.when(inside(v, f, dv, df, V, F))
        def _():
            remote(a, b, sends.at[n], recvs.at[n], v + dv, f + df).wait_send()

        @pl.when(inside(v, f, -dv, -df, V, F))
        def _():
            remote(a, b, sends.at[n], recvs.at[n], v - dv, f - df).wait_recv()


def greet_sides(v, f, V, F):
    count = 0
    for dv, df in SIDES:
        ok = inside(v, f, dv, df, V, F)

        @pl.when(ok)
        def _():
            signal(v + dv, f + df)

        count = count + ok.astype(jnp.int32)
    return count


def whole_kernel(
    V, F,
    vol, cot, fk, kk,
    out, gc_out, gf_out,
    w, ck, rk, total, rp, rin, vpad, cpad, sh, mask, ppad, psh, csh, gc, gf, co, g, slots, red,
    vs, vr, cs, cr, ts, tr, ps, pr, os, orr, ss, rs, ls,
):
    v, f = place()
    n = V * F
    me = v * F + f
    planes, frows, chans, cols = vol.shape
    half = cols // 2
    rows = frows // 2
    filters = co.shape[2]
    outs = filters * F
    chunk = red.shape[0]

    def peer_of(d):
        p = lax.rem(me + d, n)
        return p, p // F, lax.rem(p, F)

    def greet(d, c):
        _, pv, pf = peer_of(d)
        signal(pv, pf)
        return c

    lax.fori_loop(1, n, greet, 0)

    x = lax.broadcasted_iota(jnp.int32, (cols, cols), 0)
    y = lax.broadcasted_iota(jnp.int32, (cols, cols), 1)
    home = jnp.where(y < half, 2 * y, 2 * (y - half) + 1)
    x1 = lax.broadcasted_iota(jnp.int32, (half, half), 0)
    y1 = lax.broadcasted_iota(jnp.int32, (half, half), 1)

    def pick2(s):
        return jnp.where(x == home + (s - 1), 1.0, 0.0).astype(BF16)

    def pick1(s):
        return jnp.where(x1 == y1 + (s - 1), 1.0, 0.0).astype(BF16)

    def shift_fine(p, r, block):
        flat = block.reshape(-1, cols)
        for s in range(3):
            sh[s, p, r] = dot(flat, pick2(s)).astype(BF16).reshape(block.shape)

    for p in range(planes):
        shift_fine(1 + p, pl.ds(1, frows), vol[p])
    blank = jnp.zeros((chans, chans), BF16)
    for p in range(2):
        for r in range(2):
            row = []
            for s in range(3):
                for a in range(4):
                    for b in range(4):
                        ok = 0 <= a - p < 3 and 0 <= b - r < 3
                        row.append(fk[a - p, b - r, s] if ok else blank)
            q = (2 * p + r) * chans
            w[q : q + chans, :] = jnp.concatenate(row, axis=1)
    span = [(s, a, b) for s in range(3) for a in range(3) for b in range(3)]
    kt = jnp.concatenate([kk[a, b, s] for s, a, b in span], axis=0)
    eye = jnp.where(
        lax.broadcasted_iota(jnp.int32, (outs, outs), 0)
        == lax.broadcasted_iota(jnp.int32, (outs, outs), 1),
        1.0,
        0.0,
    ).astype(BF16)
    ck[...] = dot_t(eye, kt).astype(BF16)
    for a in range(3):
        row = [kk[a, 2 - b, 2 - s] for s in range(3) for b in range(3)]
        rk[a * chans : (a + 1) * chans, :] = jnp.concatenate(row, axis=1)
    gc[...] = jnp.zeros(gc.shape, F32)
    gf[...] = jnp.zeros(gf.shape, F32)
    g[...] = jnp.zeros(g.shape, g.dtype)

    pl.semaphore_wait(pltpu.get_barrier_semaphore(), n - 1)

    halo_start(vol, vpad, vs, vr, v, f, V, F)
    copies = []
    for d in range(1, F):
        far = lax.rem(f + d, F)
        copies.append(
            remote(cot.at[pl.ds(far * rows, rows + 2)], cpad.at[f], cs.at[d], cr.at[d], v, far)
        )
        copies[-1].start()
    mine = pltpu.make_async_copy(cot.at[pl.ds(f * rows, rows + 2)], cpad.at[f], ls.at[0])
    mine.start()
    for side in (0, 1):

        @pl.when(v == (0 if side == 0 else V - 1))
        def _():
            rin[side] = jnp.zeros(rin.shape[1:], rin.dtype)

    halo_wait(vol, vpad, vs, vr, v, f, V, F)
    for p in (0, planes + 1):
        shift_fine(p, pl.ds(0, frows + 2), vpad[p])
    for r in (0, frows + 1):
        shift_fine(pl.ds(1, planes), r, vpad[pl.ds(1, planes), r])

    def fine(r, c):
        d = sh[:, :, pl.ds(2 * r, 4)].reshape(w.shape[1], cols)
        pre = dot(w[...], d)
        mask[r] = jnp.where(pre > 0, 1.0, 0.0).astype(BF16)
        act = jnp.maximum(pre, 0.0)
        s4 = act[0:chans] + act[chans : 2 * chans] + act[2 * chans : 3 * chans] + act[3 * chans :]
        ppad[1, 1 + r] = ((s4[:, :half] + s4[:, half:]) * 0.125).astype(BF16)
        return c

    lax.fori_loop(0, rows // 2, fine, 0, unroll=4)
    mine.wait()
    for c in copies:
        c.wait_recv()
    for k in range(F):
        b = cpad[k]
        for s in range(3):
            m = b
            if s != 1:
                m = dot(b.reshape(-1, half), pick1(s)).astype(BF16).reshape(b.shape)
            csh[s, :, pl.ds(k * filters, filters)] = m

    def parts(t, c):
        r = 2 * t
        one = csh[:, pl.ds(r, 3)].reshape(rk.shape[1], half)
        two = csh[:, pl.ds(r + 1, 3)].reshape(rk.shape[1], half)
        both = dot(rk[...], jnp.concatenate([one, two], axis=1))
        for a in range(3):
            rp[a, r] = both[a * chans : (a + 1) * chans, :half]
            rp[a, r + 1] = both[a * chans : (a + 1) * chans, half:]
        return c

    lax.fori_loop(0, rows // 2, parts, 0, unroll=2)
    for side, dv in ((0, 1), (1, -1)):

        @pl.when(inside(v, f, dv, 0, V, F))
        def _():
            remote(rp.at[1 + dv], rin.at[side], ts.at[side], tr.at[side], v + dv, f).start()

    lax.fori_loop(rows // 2, rows, fine, 0, unroll=4)

    own = ppad.at[pl.ds(1, 1), pl.ds(1, rows)]
    halo_start(own, ppad, ps, pr, v, f, V, F)

    for c in copies:
        c.wait_send()
    for side, dv in ((0, 1), (1, -1)):
        c = remote(rp.at[1 + dv], rin.at[side], ts.at[side], tr.at[side], v, f)

        @pl.when(inside(v, f, dv, 0, V, F))
        def _():
            c.wait_send()

        @pl.when(inside(v, f, -dv, 0, V, F))
        def _():
            c.wait_recv()

    def pair(ref, r, size):
        one = ref[:, :, pl.ds(r, 3)].reshape(size, half)
        two = ref[:, :, pl.ds(r + 1, 3)].reshape(size, half)
        return jnp.concatenate([one, two], axis=1)

    def back(r, c):
        ret = ((rp[1, r] + rin[0, r] + rin[1, r]) * 0.125).astype(BF16)
        wide = jnp.concatenate([ret, ret], axis=1)
        fc = jnp.concatenate([wide] * 4, axis=0) * mask[r]
        d = sh[:, :, pl.ds(2 * r, 4)].reshape(48 * chans, cols)
        gf[...] += dot_t(d, fc)
        return c

    lax.fori_loop(0, rows, back, 0, unroll=2)
    full = gf[...].reshape(3, 4, 4, chans, 4 * chans)
    sums = None
    for p in range(2):
        for r in range(2):
            q = (2 * p + r) * chans
            part = full[:, p : p + 3, r : r + 3].reshape(27 * chans, 4 * chans)[:, q : q + chans]
            sums = part if sums is None else sums + part
    taps = gc.shape[0]
    g[0:taps, outs : outs + chans] = sums.astype(g.dtype)

    halo_wait(own, ppad, ps, pr, v, f, V, F)
    for p in range(3):
        a = ppad[p]
        for s in range(3):
            m = a
            if s != 1:
                m = dot(a.reshape(-1, half), pick1(s)).astype(BF16).reshape(a.shape)
            psh[s, p] = m

    def coarse_grad(t, c):
        r = 2 * t
        both = jnp.concatenate([csh[1, r + 1], csh[1, r + 2]], axis=1)
        gc[...] += dot_t(pair(psh, r, taps), both)
        return c

    lax.fori_loop(0, rows // 2, coarse_grad, 0, unroll=2)
    g[0:taps, 0:outs] = gc[...].astype(g.dtype)

    def scatter(d, c):
        p, pv, pf = peer_of(d)
        src = g.at[pl.ds(pl.multiple_of(p * chunk, chunk), chunk)]
        remote(src, slots.at[d - 1], ss.at[0], rs.at[0], pv, pf).start()
        return c

    lax.fori_loop(1, n, scatter, 0)

    def coarse(t, c):
        r = 2 * t
        o = dot(ck[...], pair(psh, r, taps)).astype(BF16)
        co[:, r] = o[:, :half].reshape(F, filters, half)
        co[:, r + 1] = o[:, half:].reshape(F, filters, half)
        return c

    lax.fori_loop(0, rows // 2, coarse, 0, unroll=2)
    mine = pltpu.make_async_copy(co.at[f], out.at[pl.ds(f * rows, rows)], ls.at[1])
    mine.start()
    copies = []
    for d in range(1, F):
        far = lax.rem(f + d, F)
        copies.append(remote(co.at[far], out.at[pl.ds(f * rows, rows)], os.at[d], orr.at[d], v, far))
        copies[-1].start()
    pltpu.make_async_copy(slots, slots, rs.at[0]).wait()
    here = pl.ds(pl.multiple_of(me * chunk, chunk), chunk)
    red[...] = (g[here].astype(F32) + jnp.sum(slots[...].astype(F32), axis=0)).astype(red.dtype)
    total[here] = red[...]

    def gather(d, c):
        _, pv, pf = peer_of(d)
        remote(red, total.at[here], ss.at[1], rs.at[1], pv, pf).start()
        return c

    lax.fori_loop(1, n, gather, 0)
    mine.wait()
    for c in copies:
        c.wait()
    pltpu.make_async_copy(slots, slots, ss.at[0]).wait()
    pltpu.make_async_copy(slots, slots, rs.at[1]).wait()
    pltpu.make_async_copy(slots, slots, ss.at[1]).wait()
    for at, (s, a, b) in enumerate(span):
        block = total[at * chans : (at + 1) * chans, :].astype(F32)
        gc_out[a, b, s] = block[:, :outs]
        gf_out[a, b, s] = block[:, outs : outs + chans]


def local(V, F, volume, fine_kernel, coarse_kernel, coarse_cot):
    chans, planes, frows, cols = volume.shape
    filters, _, allrows, half = coarse_cot.shape
    rows = allrows // F
    outs = filters * F
    n = V * F
    taps = 27 * chans
    chunk = 16 * (-(-taps // (16 * n)))
    vmem = pl.BlockSpec(memory_space=pltpu.VMEM)
    dma = pltpu.SemaphoreType.DMA

    def call(body, ins, outputs, scratch, ident=None):
        extra = {} if ident is None else dict(collective_id=ident, has_side_effects=True)
        return pl.pallas_call(
            body,
            out_shape=[jax.ShapeDtypeStruct(s, t) for s, t in outputs],
            in_specs=[vmem] * ins,
            out_specs=[vmem] * len(outputs),
            scratch_shapes=scratch,
            compiler_params=pltpu.CompilerParams(vmem_limit_bytes=56 * 2**20, **extra),
        )

    vol_t = volume.transpose(1, 2, 0, 3)
    cot_t = jnp.pad(coarse_cot[:, 0].transpose(1, 0, 2), ((1, 1), (0, 0), (0, 0)))
    fk = fine_kernel.transpose(2, 3, 4, 0, 1)
    kk = coarse_kernel.transpose(2, 3, 4, 1, 0)
    out, gc, gf = call(
        functools.partial(whole_kernel, V, F),
        4,
        [
            ((allrows, filters, half), BF16),
            ((3, 3, 3, chans, outs), F32),
            ((3, 3, 3, chans, chans), F32),
        ],
        [
            pltpu.VMEM((4 * chans, 48 * chans), BF16),
            pltpu.VMEM((outs, taps), BF16),
            pltpu.VMEM((3 * chans, 9 * outs), BF16),
            pltpu.VMEM((n * chunk, 128), BF16),
            pltpu.VMEM((3, rows, chans, half), F32),
            pltpu.VMEM((2, rows, chans, half), F32),
            pltpu.VMEM((planes + 2, frows + 2, chans, cols), BF16),
            pltpu.VMEM((F, rows + 2, filters, half), BF16),
            pltpu.VMEM((3, planes + 2, frows + 2, chans, cols), BF16),
            pltpu.VMEM((rows, 4 * chans, cols), BF16),
            pltpu.VMEM((3, rows + 2, chans, half), BF16),
            pltpu.VMEM((3, 3, rows + 2, chans, half), BF16),
            pltpu.VMEM((3, rows + 2, outs, half), BF16),
            pltpu.VMEM((taps, outs), F32),
            pltpu.VMEM((48 * chans, 4 * chans), F32),
            pltpu.VMEM((F, rows, filters, half), BF16),
            pltpu.VMEM((n * chunk, 128), BF16),
            pltpu.VMEM((n - 1, chunk, 128), BF16),
            pltpu.VMEM((chunk, 128), BF16),
        ]
        + [dma((k,)) for k in (8, 8, F, F, 2, 2, 8, 8, F, F, 2, 2, 2)],
        0,
    )(vol_t, cot_t, fk, kk)
    coarse_out = out.transpose(1, 0, 2)[:, None]
    return coarse_out, gf.transpose(4, 3, 0, 1, 2), gc.transpose(4, 3, 0, 1, 2)


def solution(mesh):
    from jax.sharding import PartitionSpec as P

    in_specs = (P(None, "vox", "fil", None), P(), P(), P("fil", "vox", None, None))
    out_specs = (P("fil", "vox", None, None), P(), P())
    body = functools.partial(local, mesh.shape["vox"], mesh.shape["fil"])
    return jax.shard_map(body, mesh=mesh, in_specs=in_specs, out_specs=out_specs, check_vma=False)
```

```python
import functools

import jax
import jax.numpy as jnp
from jax import lax
from jax.experimental import pallas as pl
from jax.experimental.pallas import tpu as pltpu

F32 = jnp.float32
BF16 = jnp.bfloat16
MESH = pl.DeviceIdType.MESH
SIDES = [(dv, df) for dv in (-1, 0, 1) for df in (-1, 0, 1) if (dv, df) != (0, 0)]


def dot(a, b):
    return jnp.dot(a, b, preferred_element_type=F32)


def dot_t(a, b):
    return lax.dot_general(a, b, (((1,), (1,)), ((), ())), preferred_element_type=F32)


def place():
    return lax.axis_index("vox"), lax.axis_index("fil")


def inside(v, f, dv, df, V, F):
    ok = None
    for at, step, size in ((v, dv, V), (f, df, F)):
        if step:
            here = (at + step >= 0) & (at + step < size)
            ok = here if ok is None else ok & here
    return ok


def remote(src, dst, send, recv, v, f):
    return pltpu.make_async_remote_copy(
        src_ref=src,
        dst_ref=dst,
        send_sem=send,
        recv_sem=recv,
        device_id={"vox": v, "fil": f},
        device_id_type=MESH,
    )


def signal(v, f):
    pl.semaphore_signal(
        pltpu.get_barrier_semaphore(), inc=1, device_id={"vox": v, "fil": f}, device_id_type=MESH
    )


def halo_views(dv, df, src, dst, planes, rows):
    sp = {1: pl.ds(planes - 1, 1), 0: pl.ds(0, planes), -1: pl.ds(0, 1)}[dv]
    dp = {1: pl.ds(0, 1), 0: pl.ds(1, planes), -1: pl.ds(planes + 1, 1)}[dv]
    sr = {1: pl.ds(rows - 1, 1), 0: pl.ds(0, rows), -1: pl.ds(0, 1)}[df]
    dr = {1: pl.ds(0, 1), 0: pl.ds(1, rows), -1: pl.ds(rows + 1, 1)}[df]
    return src.at[sp, sr], dst.at[dp, dr]


def halo_start(src, dst, sends, recvs, v, f, V, F):
    planes, rows = src.shape[:2]
    for n, (dv, df) in enumerate(SIDES):
        a, b = halo_views(dv, df, src, dst, planes, rows)

        @pl.when(inside(v, f, dv, df, V, F))
        def _():
            remote(a, b, sends.at[n], recvs.at[n], v + dv, f + df).start()

        @pl.when(jnp.logical_not(inside(v, f, -dv, -df, V, F)))
        def _():
            b[...] = jnp.zeros(b.shape, b.dtype)


def halo_wait(src, dst, sends, recvs, v, f, V, F):
    planes, rows = src.shape[:2]
    for n, (dv, df) in enumerate(SIDES):
        a, b = halo_views(dv, df, src, dst, planes, rows)

        @pl.when(inside(v, f, dv, df, V, F))
        def _():
            remote(a, b, sends.at[n], recvs.at[n], v + dv, f + df).wait_send()

        @pl.when(inside(v, f, -dv, -df, V, F))
        def _():
            remote(a, b, sends.at[n], recvs.at[n], v - dv, f - df).wait_recv()


def greet_sides(v, f, V, F):
    count = 0
    for dv, df in SIDES:
        ok = inside(v, f, dv, df, V, F)

        @pl.when(ok)
        def _():
            signal(v + dv, f + df)

        count = count + ok.astype(jnp.int32)
    return count


def whole_kernel(
    V, F,
    vol_hbm, cot_hbm, fk_hbm, kk_hbm,
    out, gc_out, gf_out,
    vol_in, cot_in, fk, kk, vol, cot, cor, w, ck, rk, total, rp, rin, vpad, cpad, sh, mask, ppad, psh, csh, gc, gf, co, g, slots, red,
    vs, vr, cs, cr, ts, tr, ps, pr, os, orr, ss, rs, ls, ins,
):
    v, f = place()
    n = V * F
    me = v * F + f
    planes, frows, chans, cols = vol.shape
    half = cols // 2
    rows = frows // 2
    filters = co.shape[1]
    outs = filters * F
    chunk = red.shape[0]

    def peer_of(d):
        p = lax.rem(me + d, n)
        return p, p // F, lax.rem(p, F)

    def greet(d, c):
        _, pv, pf = peer_of(d)
        signal(pv, pf)
        return c

    pairs = ((vol_hbm, vol_in), (cot_hbm, cot_in), (fk_hbm, fk), (kk_hbm, kk))
    loads = [pltpu.make_async_copy(a, b, ins.at[k]) for k, (a, b) in enumerate(pairs)]
    for c in loads:
        c.start()
    lax.fori_loop(1, n, greet, 0)
    loads[0].wait()
    for p in range(planes):
        vol[p] = jnp.transpose(vol_in[:, p].astype(F32), (1, 0, 2)).astype(BF16)
    height = cot_in.shape[2]
    loads[1].wait()
    for edge in (0, height + 1):
        cot[edge] = jnp.zeros(cot.shape[1:], BF16)
    cot[pl.ds(1, height)] = jnp.transpose(cot_in[:, 0].astype(F32), (1, 0, 2)).astype(BF16)

    x = lax.broadcasted_iota(jnp.int32, (cols, cols), 0)
    y = lax.broadcasted_iota(jnp.int32, (cols, cols), 1)
    home = jnp.where(y < half, 2 * y, 2 * (y - half) + 1)
    x1 = lax.broadcasted_iota(jnp.int32, (half, half), 0)
    y1 = lax.broadcasted_iota(jnp.int32, (half, half), 1)

    def pick2(s):
        return jnp.where(x == home + (s - 1), 1.0, 0.0).astype(BF16)

    def pick1(s):
        return jnp.where(x1 == y1 + (s - 1), 1.0, 0.0).astype(BF16)

    def shift_fine(p, r, block):
        flat = block.reshape(-1, cols)
        for s in range(3):
            sh[s, p, r] = dot(flat, pick2(s)).astype(BF16).reshape(block.shape)

    pl.semaphore_wait(pltpu.get_barrier_semaphore(), n - 1)

    halo_start(vol, vpad, vs, vr, v, f, V, F)
    copies = []
    for d in range(1, F):
        far = lax.rem(f + d, F)
        copies.append(
            remote(cot.at[pl.ds(far * rows, rows + 2)], cpad.at[f], cs.at[d], cr.at[d], v, far)
        )
        copies[-1].start()
    mine = pltpu.make_async_copy(cot.at[pl.ds(f * rows, rows + 2)], cpad.at[f], ls.at[0])
    mine.start()
    for side in (0, 1):

        @pl.when(v == (0 if side == 0 else V - 1))
        def _():
            rin[side] = jnp.zeros(rin.shape[1:], rin.dtype)

    for p in range(planes):
        shift_fine(1 + p, pl.ds(1, frows), vol[p])
    loads[2].wait()
    loads[3].wait()
    blank = jnp.zeros((chans, chans), BF16)
    for p in range(2):
        for r in range(2):
            row = []
            for s in range(3):
                for a in range(4):
                    for b in range(4):
                        ok = 0 <= a - p < 3 and 0 <= b - r < 3
                        row.append(fk[a - p, b - r, s] if ok else blank)
            q = (2 * p + r) * chans
            w[q : q + chans, :] = jnp.concatenate(row, axis=1)
    span = [(s, a, b) for s in range(3) for a in range(3) for b in range(3)]
    kt = jnp.concatenate([kk[a, b, s] for s, a, b in span], axis=0)
    eye = jnp.where(
        lax.broadcasted_iota(jnp.int32, (outs, outs), 0)
        == lax.broadcasted_iota(jnp.int32, (outs, outs), 1),
        1.0,
        0.0,
    ).astype(BF16)
    ck[...] = dot_t(eye, kt).astype(BF16)
    for a in range(3):
        row = [kk[a, 2 - b, 2 - s] for s in range(3) for b in range(3)]
        rk[a * chans : (a + 1) * chans, :] = jnp.concatenate(row, axis=1)
    gc[...] = jnp.zeros(gc.shape, F32)
    gf[...] = jnp.zeros(gf.shape, F32)
    g[...] = jnp.zeros(g.shape, g.dtype)

    halo_wait(vol, vpad, vs, vr, v, f, V, F)
    for p in (0, planes + 1):
        shift_fine(p, pl.ds(0, frows + 2), vpad[p])
    for r in (0, frows + 1):
        shift_fine(pl.ds(1, planes), r, vpad[pl.ds(1, planes), r])

    def fine(r, c):
        d = sh[:, :, pl.ds(2 * r, 4)].reshape(w.shape[1], cols)
        pre = dot(w[...], d)
        mask[r] = jnp.where(pre > 0, 1.0, 0.0).astype(BF16)
        act = jnp.maximum(pre, 0.0)
        s4 = act[0:chans] + act[chans : 2 * chans] + act[2 * chans : 3 * chans] + act[3 * chans :]
        ppad[1, 1 + r] = ((s4[:, :half] + s4[:, half:]) * 0.125).astype(BF16)
        return c

    lax.fori_loop(0, rows // 2, fine, 0, unroll=4)
    mine.wait()
    for c in copies:
        c.wait_recv()
    for k in range(F):
        b = cpad[k]
        for s in range(3):
            m = b
            if s != 1:
                m = dot(b.reshape(-1, half), pick1(s)).astype(BF16).reshape(b.shape)
            csh[s, :, pl.ds(k * filters, filters)] = m

    def parts(t, c):
        r = 2 * t
        one = csh[:, pl.ds(r, 3)].reshape(rk.shape[1], half)
        two = csh[:, pl.ds(r + 1, 3)].reshape(rk.shape[1], half)
        both = dot(rk[...], jnp.concatenate([one, two], axis=1))
        for a in range(3):
            rp[a, r] = both[a * chans : (a + 1) * chans, :half]
            rp[a, r + 1] = both[a * chans : (a + 1) * chans, half:]
        return c

    lax.fori_loop(0, rows // 2, parts, 0, unroll=2)
    for side, dv in ((0, 1), (1, -1)):

        @pl.when(inside(v, f, dv, 0, V, F))
        def _():
            remote(rp.at[1 + dv], rin.at[side], ts.at[side], tr.at[side], v + dv, f).start()

    lax.fori_loop(rows // 2, rows, fine, 0, unroll=4)

    own = ppad.at[pl.ds(1, 1), pl.ds(1, rows)]
    halo_start(own, ppad, ps, pr, v, f, V, F)

    for c in copies:
        c.wait_send()
    for side, dv in ((0, 1), (1, -1)):
        c = remote(rp.at[1 + dv], rin.at[side], ts.at[side], tr.at[side], v, f)

        @pl.when(inside(v, f, dv, 0, V, F))
        def _():
            c.wait_send()

        @pl.when(inside(v, f, -dv, 0, V, F))
        def _():
            c.wait_recv()

    def pair(ref, r, size):
        one = ref[:, :, pl.ds(r, 3)].reshape(size, half)
        two = ref[:, :, pl.ds(r + 1, 3)].reshape(size, half)
        return jnp.concatenate([one, two], axis=1)

    def back(r, c):
        ret = ((rp[1, r] + rin[0, r] + rin[1, r]) * 0.125).astype(BF16)
        wide = jnp.concatenate([ret, ret], axis=1)
        fc = jnp.concatenate([wide] * 4, axis=0) * mask[r]
        d = sh[:, :, pl.ds(2 * r, 4)].reshape(48 * chans, cols)
        gf[...] += dot_t(d, fc)
        return c

    lax.fori_loop(0, rows, back, 0, unroll=2)
    full = gf[...].reshape(3, 4, 4, chans, 4 * chans)
    sums = None
    for p in range(2):
        for r in range(2):
            q = (2 * p + r) * chans
            part = full[:, p : p + 3, r : r + 3].reshape(27 * chans, 4 * chans)[:, q : q + chans]
            sums = part if sums is None else sums + part
    taps = gc.shape[0]
    g[0:taps, outs : outs + chans] = sums.astype(g.dtype)

    halo_wait(own, ppad, ps, pr, v, f, V, F)
    for p in range(3):
        a = ppad[p]
        for s in range(3):
            m = a
            if s != 1:
                m = dot(a.reshape(-1, half), pick1(s)).astype(BF16).reshape(a.shape)
            psh[s, p] = m

    def coarse_grad(t, c):
        r = 2 * t
        both = jnp.concatenate([csh[1, r + 1], csh[1, r + 2]], axis=1)
        gc[...] += dot_t(pair(psh, r, taps), both)
        return c

    lax.fori_loop(0, rows // 2, coarse_grad, 0, unroll=2)
    g[0:taps, 0:outs] = gc[...].astype(g.dtype)

    def scatter(d, c):
        p, pv, pf = peer_of(d)
        src = g.at[pl.ds(pl.multiple_of(p * chunk, chunk), chunk)]
        remote(src, slots.at[d - 1], ss.at[0], rs.at[0], pv, pf).start()
        return c

    lax.fori_loop(1, n, scatter, 0)

    def coarse(t, c):
        r = 2 * t
        o = dot(ck[...], pair(psh, r, taps))
        cor[r] = o[:, :half]
        cor[r + 1] = o[:, half:]
        return c

    lax.fori_loop(0, rows // 2, coarse, 0, unroll=2)
    co[...] = jnp.transpose(cor[...], (1, 0, 2)).astype(BF16).reshape(co.shape)
    spot = out.at[:, pl.ds(pl.multiple_of(f * rows, rows), rows)]
    mine = pltpu.make_async_copy(co.at[f], spot, ls.at[1])
    mine.start()
    copies = []
    for d in range(1, F):
        far = lax.rem(f + d, F)
        copies.append(remote(co.at[far], spot, os.at[d], orr.at[d], v, far))
        copies[-1].start()
    pltpu.make_async_copy(slots, slots, rs.at[0]).wait()
    here = pl.ds(pl.multiple_of(me * chunk, chunk), chunk)
    red[...] = (g[here].astype(F32) + jnp.sum(slots[...].astype(F32), axis=0)).astype(red.dtype)
    total[here] = red[...]

    def gather(d, c):
        _, pv, pf = peer_of(d)
        remote(red, total.at[here], ss.at[1], rs.at[1], pv, pf).start()
        return c

    lax.fori_loop(1, n, gather, 0)
    mine.wait()
    for c in copies:
        c.wait()
    pltpu.make_async_copy(slots, slots, ss.at[0]).wait()
    pltpu.make_async_copy(slots, slots, rs.at[1]).wait()
    pltpu.make_async_copy(slots, slots, ss.at[1]).wait()
    for at, (s, a, b) in enumerate(span):
        block = total[at * chans : (at + 1) * chans, :].astype(F32)
        gc_out[a, b, s] = block[:, :outs]
        gf_out[a, b, s] = block[:, outs : outs + chans]


def local(V, F, volume, fine_kernel, coarse_kernel, coarse_cot):
    chans, planes, frows, cols = volume.shape
    filters, _, allrows, half = coarse_cot.shape
    rows = allrows // F
    outs = filters * F
    n = V * F
    taps = 27 * chans
    chunk = 16 * (-(-taps // (16 * n)))
    vmem = pl.BlockSpec(memory_space=pltpu.VMEM)
    dma = pltpu.SemaphoreType.DMA

    def call(body, ins, outputs, scratch, ident=None):
        extra = {} if ident is None else dict(collective_id=ident, has_side_effects=True)
        return pl.pallas_call(
            body,
            out_shape=[jax.ShapeDtypeStruct(s, t) for s, t in outputs],
            in_specs=[pl.BlockSpec(memory_space=pltpu.HBM)] * ins,
            out_specs=[vmem] * len(outputs),
            scratch_shapes=scratch,
            compiler_params=pltpu.CompilerParams(vmem_limit_bytes=56 * 2**20, **extra),
        )

    fk = fine_kernel.transpose(2, 3, 4, 0, 1)
    kk = coarse_kernel.transpose(2, 3, 4, 1, 0)
    out, gc, gf = call(
        functools.partial(whole_kernel, V, F),
        4,
        [
            ((filters, allrows, half), BF16),
            ((3, 3, 3, chans, outs), F32),
            ((3, 3, 3, chans, chans), F32),
        ],
        [
            pltpu.VMEM(volume.shape, BF16),
            pltpu.VMEM(coarse_cot.shape, BF16),
            pltpu.VMEM(fk.shape, BF16),
            pltpu.VMEM(kk.shape, BF16),
            pltpu.VMEM((planes, frows, chans, cols), BF16),
            pltpu.VMEM((allrows + 2, filters, half), BF16),
            pltpu.VMEM((rows, outs, half), F32),
            pltpu.VMEM((4 * chans, 48 * chans), BF16),
            pltpu.VMEM((outs, taps), BF16),
            pltpu.VMEM((3 * chans, 9 * outs), BF16),
            pltpu.VMEM((n * chunk, 128), BF16),
            pltpu.VMEM((3, rows, chans, half), F32),
            pltpu.VMEM((2, rows, chans, half), F32),
            pltpu.VMEM((planes + 2, frows + 2, chans, cols), BF16),
            pltpu.VMEM((F, rows + 2, filters, half), BF16),
            pltpu.VMEM((3, planes + 2, frows + 2, chans, cols), BF16),
            pltpu.VMEM((rows, 4 * chans, cols), BF16),
            pltpu.VMEM((3, rows + 2, chans, half), BF16),
            pltpu.VMEM((3, 3, rows + 2, chans, half), BF16),
            pltpu.VMEM((3, rows + 2, outs, half), BF16),
            pltpu.VMEM((taps, outs), F32),
            pltpu.VMEM((48 * chans, 4 * chans), F32),
            pltpu.VMEM((F, filters, rows, half), BF16),
            pltpu.VMEM((n * chunk, 128), BF16),
            pltpu.VMEM((n - 1, chunk, 128), BF16),
            pltpu.VMEM((chunk, 128), BF16),
        ]
        + [dma((k,)) for k in (8, 8, F, F, 2, 2, 8, 8, F, F, 2, 2, 2, 4)],
        0,
    )(volume, coarse_cot, fk, kk)
    coarse_out = out[:, None]
    return coarse_out, gf.transpose(4, 3, 0, 1, 2), gc.transpose(4, 3, 0, 1, 2)


def solution(mesh):
    from jax.sharding import PartitionSpec as P

    in_specs = (P(None, "vox", "fil", None), P(), P(), P("fil", "vox", None, None))
    out_specs = (P("fil", "vox", None, None), P(), P())
    body = functools.partial(local, mesh.shape["vox"], mesh.shape["fil"])
    return jax.shard_map(body, mesh=mesh, in_specs=in_specs, out_specs=out_specs, check_vma=False)
```

```python
import functools

import jax
import jax.numpy as jnp
from jax import lax
from jax.experimental import pallas as pl
from jax.experimental.pallas import tpu as pltpu

F32 = jnp.float32
BF16 = jnp.bfloat16
MESH = pl.DeviceIdType.MESH
SIDES = [(dv, df) for dv in (-1, 0, 1) for df in (-1, 0, 1) if (dv, df) != (0, 0)]


def dot(a, b):
    return jnp.dot(a, b, preferred_element_type=F32)


def dot_t(a, b):
    return lax.dot_general(a, b, (((1,), (1,)), ((), ())), preferred_element_type=F32)


def place():
    return lax.axis_index("vox"), lax.axis_index("fil")


def inside(v, f, dv, df, V, F):
    ok = None
    for at, step, size in ((v, dv, V), (f, df, F)):
        if step:
            here = (at + step >= 0) & (at + step < size)
            ok = here if ok is None else ok & here
    return ok


def remote(src, dst, send, recv, v, f):
    return pltpu.make_async_remote_copy(
        src_ref=src,
        dst_ref=dst,
        send_sem=send,
        recv_sem=recv,
        device_id={"vox": v, "fil": f},
        device_id_type=MESH,
    )


def signal(v, f):
    pl.semaphore_signal(
        pltpu.get_barrier_semaphore(), inc=1, device_id={"vox": v, "fil": f}, device_id_type=MESH
    )


def halo_views(dv, df, src, dst, planes, rows):
    sp = {1: pl.ds(planes - 1, 1), 0: pl.ds(0, planes), -1: pl.ds(0, 1)}[dv]
    dp = {1: pl.ds(0, 1), 0: pl.ds(1, planes), -1: pl.ds(planes + 1, 1)}[dv]
    sr = {1: pl.ds(rows - 1, 1), 0: pl.ds(0, rows), -1: pl.ds(0, 1)}[df]
    dr = {1: pl.ds(0, 1), 0: pl.ds(1, rows), -1: pl.ds(rows + 1, 1)}[df]
    return src.at[sp, sr], dst.at[dp, dr]


def halo_start(src, dst, sends, recvs, v, f, V, F):
    planes, rows = src.shape[:2]
    for n, (dv, df) in enumerate(SIDES):
        a, b = halo_views(dv, df, src, dst, planes, rows)

        @pl.when(inside(v, f, dv, df, V, F))
        def _():
            remote(a, b, sends.at[n], recvs.at[n], v + dv, f + df).start()

        @pl.when(jnp.logical_not(inside(v, f, -dv, -df, V, F)))
        def _():
            b[...] = jnp.zeros(b.shape, b.dtype)


def halo_wait(src, dst, sends, recvs, v, f, V, F):
    planes, rows = src.shape[:2]
    for n, (dv, df) in enumerate(SIDES):
        a, b = halo_views(dv, df, src, dst, planes, rows)

        @pl.when(inside(v, f, dv, df, V, F))
        def _():
            remote(a, b, sends.at[n], recvs.at[n], v + dv, f + df).wait_send()

        @pl.when(inside(v, f, -dv, -df, V, F))
        def _():
            remote(a, b, sends.at[n], recvs.at[n], v - dv, f - df).wait_recv()


def greet_sides(v, f, V, F):
    count = 0
    for dv, df in SIDES:
        ok = inside(v, f, dv, df, V, F)

        @pl.when(ok)
        def _():
            signal(v + dv, f + df)

        count = count + ok.astype(jnp.int32)
    return count


def whole_kernel(
    V, F,
    vol_hbm, cot_hbm, fk_hbm, kk_hbm,
    out, gc_out, gf_out,
    vol_in, cot_in, fk, kk, vol, cot, cor, w, ck, rk, total, rp, rin, vpad, cpad, sh, mask, ppad, psh, csh, gc, gf, co, g, slots, red,
    vs, vr, cs, cr, ts, tr, ps, pr, os, orr, ss, rs, ls, ins,
):
    v, f = place()
    n = V * F
    me = v * F + f
    planes, frows, chans, cols = vol.shape
    half = cols // 2
    rows = frows // 2
    filters = co.shape[1]
    outs = filters * F
    chunk = red.shape[0]

    def peer_of(d):
        p = lax.rem(me + d, n)
        return p, p // F, lax.rem(p, F)

    def greet(d, c):
        _, pv, pf = peer_of(d)
        signal(pv, pf)
        return c

    pairs = ((vol_hbm, vol_in), (cot_hbm, cot_in), (fk_hbm, fk), (kk_hbm, kk))
    loads = [pltpu.make_async_copy(a, b, ins.at[k]) for k, (a, b) in enumerate(pairs)]
    for c in loads:
        c.start()
    lax.fori_loop(1, n, greet, 0)
    loads[0].wait()
    for p in range(planes):
        vol[p] = jnp.transpose(vol_in[:, p].astype(F32), (1, 0, 2)).astype(BF16)
    height = cot_in.shape[2]
    loads[1].wait()
    for edge in (0, height + 1):
        cot[edge] = jnp.zeros(cot.shape[1:], BF16)
    cot[pl.ds(1, height)] = jnp.transpose(cot_in[:, 0].astype(F32), (1, 0, 2)).astype(BF16)

    x = lax.broadcasted_iota(jnp.int32, (cols, cols), 0)
    y = lax.broadcasted_iota(jnp.int32, (cols, cols), 1)
    home = jnp.where(y < half, 2 * y, 2 * (y - half) + 1)
    x1 = lax.broadcasted_iota(jnp.int32, (half, half), 0)
    y1 = lax.broadcasted_iota(jnp.int32, (half, half), 1)

    def pick2(s):
        return jnp.where(x == home + (s - 1), 1.0, 0.0).astype(BF16)

    def pick1(s):
        return jnp.where(x1 == y1 + (s - 1), 1.0, 0.0).astype(BF16)

    def shift_fine(p, r, block):
        flat = block.reshape(-1, cols)
        for s in range(3):
            sh[s, p, r] = dot(flat, pick2(s)).astype(BF16).reshape(block.shape)

    pl.semaphore_wait(pltpu.get_barrier_semaphore(), n - 1)

    halo_start(vol, vpad, vs, vr, v, f, V, F)
    copies = []
    for d in range(1, F):
        far = lax.rem(f + d, F)
        copies.append(
            remote(cot.at[pl.ds(far * rows, rows + 2)], cpad.at[f], cs.at[d], cr.at[d], v, far)
        )
        copies[-1].start()
    mine = pltpu.make_async_copy(cot.at[pl.ds(f * rows, rows + 2)], cpad.at[f], ls.at[0])
    mine.start()
    for side in (0, 1):

        @pl.when(v == (0 if side == 0 else V - 1))
        def _():
            rin[side] = jnp.zeros(rin.shape[1:], rin.dtype)

    for p in range(planes):
        shift_fine(1 + p, pl.ds(1, frows), vol[p])
    loads[2].wait()
    loads[3].wait()
    blank = jnp.zeros((chans, chans), BF16)
    for p in range(2):
        for r in range(2):
            row = []
            for s in range(3):
                for a in range(4):
                    for b in range(4):
                        ok = 0 <= a - p < 3 and 0 <= b - r < 3
                        row.append(fk[a - p, b - r, s] if ok else blank)
            q = (2 * p + r) * chans
            w[q : q + chans, :] = jnp.concatenate(row, axis=1)
    span = [(s, a, b) for s in range(3) for a in range(3) for b in range(3)]
    kt = jnp.concatenate([kk[a, b, s] for s, a, b in span], axis=0)
    eye = jnp.where(
        lax.broadcasted_iota(jnp.int32, (outs, outs), 0)
        == lax.broadcasted_iota(jnp.int32, (outs, outs), 1),
        1.0,
        0.0,
    ).astype(BF16)
    ck[...] = dot_t(eye, kt).astype(BF16)
    for a in range(3):
        row = [kk[a, 2 - b, 2 - s] for s in range(3) for b in range(3)]
        rk[a * chans : (a + 1) * chans, :] = jnp.concatenate(row, axis=1)
    gc[...] = jnp.zeros(gc.shape, F32)
    gf[...] = jnp.zeros(gf.shape, F32)
    g[...] = jnp.zeros(g.shape, g.dtype)

    halo_wait(vol, vpad, vs, vr, v, f, V, F)
    for p in (0, planes + 1):
        shift_fine(p, pl.ds(0, frows + 2), vpad[p])
    for r in (0, frows + 1):
        shift_fine(pl.ds(1, planes), r, vpad[pl.ds(1, planes), r])

    def fine(r, c):
        d = sh[:, :, pl.ds(2 * r, 4)].reshape(w.shape[1], cols)
        pre = dot(w[...], d)
        mask[r] = jnp.where(pre > 0, 1.0, 0.0).astype(BF16)
        act = jnp.maximum(pre, 0.0)
        s4 = act[0:chans] + act[chans : 2 * chans] + act[2 * chans : 3 * chans] + act[3 * chans :]
        ppad[1, 1 + r] = ((s4[:, :half] + s4[:, half:]) * 0.125).astype(BF16)
        return c

    lax.fori_loop(0, rows, fine, 0, unroll=4)

    own = ppad.at[pl.ds(1, 1), pl.ds(1, rows)]
    halo_start(own, ppad, ps, pr, v, f, V, F)

    mine.wait()
    for c in copies:
        c.wait_recv()
    for k in range(F):
        b = cpad[k]
        for s in range(3):
            m = b
            if s != 1:
                m = dot(b.reshape(-1, half), pick1(s)).astype(BF16).reshape(b.shape)
            csh[s, :, pl.ds(k * filters, filters)] = m

    def parts(t, c):
        r = 2 * t
        one = csh[:, pl.ds(r, 3)].reshape(rk.shape[1], half)
        two = csh[:, pl.ds(r + 1, 3)].reshape(rk.shape[1], half)
        both = dot(rk[...], jnp.concatenate([one, two], axis=1))
        for a in range(3):
            rp[a, r] = both[a * chans : (a + 1) * chans, :half]
            rp[a, r + 1] = both[a * chans : (a + 1) * chans, half:]
        return c

    lax.fori_loop(0, rows // 2, parts, 0, unroll=2)
    for side, dv in ((0, 1), (1, -1)):

        @pl.when(inside(v, f, dv, 0, V, F))
        def _():
            remote(rp.at[1 + dv], rin.at[side], ts.at[side], tr.at[side], v + dv, f).start()

    def pair(ref, r, size):
        one = ref[:, :, pl.ds(r, 3)].reshape(size, half)
        two = ref[:, :, pl.ds(r + 1, 3)].reshape(size, half)
        return jnp.concatenate([one, two], axis=1)

    taps = gc.shape[0]
    halo_wait(own, ppad, ps, pr, v, f, V, F)
    for p in range(3):
        a = ppad[p]
        for s in range(3):
            m = a
            if s != 1:
                m = dot(a.reshape(-1, half), pick1(s)).astype(BF16).reshape(a.shape)
            psh[s, p] = m

    def coarse_grad(t, c):
        r = 2 * t
        both = jnp.concatenate([csh[1, r + 1], csh[1, r + 2]], axis=1)
        gc[...] += dot_t(pair(psh, r, taps), both)
        return c

    lax.fori_loop(0, rows // 2, coarse_grad, 0, unroll=2)
    g[0:taps, 0:outs] = gc[...].astype(g.dtype)

    for c in copies:
        c.wait_send()
    for side, dv in ((0, 1), (1, -1)):
        c = remote(rp.at[1 + dv], rin.at[side], ts.at[side], tr.at[side], v, f)

        @pl.when(inside(v, f, dv, 0, V, F))
        def _():
            c.wait_send()

        @pl.when(inside(v, f, -dv, 0, V, F))
        def _():
            c.wait_recv()

    def back(r, c):
        ret = ((rp[1, r] + rin[0, r] + rin[1, r]) * 0.125).astype(BF16)
        wide = jnp.concatenate([ret, ret], axis=1)
        fc = jnp.concatenate([wide] * 4, axis=0) * mask[r]
        d = sh[:, :, pl.ds(2 * r, 4)].reshape(48 * chans, cols)
        gf[...] += dot_t(d, fc)
        return c

    lax.fori_loop(0, rows, back, 0, unroll=2)
    full = gf[...].reshape(3, 4, 4, chans, 4 * chans)
    sums = None
    for p in range(2):
        for r in range(2):
            q = (2 * p + r) * chans
            part = full[:, p : p + 3, r : r + 3].reshape(27 * chans, 4 * chans)[:, q : q + chans]
            sums = part if sums is None else sums + part
    g[0:taps, outs : outs + chans] = sums.astype(g.dtype)

    def scatter(d, c):
        p, pv, pf = peer_of(d)
        src = g.at[pl.ds(pl.multiple_of(p * chunk, chunk), chunk)]
        remote(src, slots.at[d - 1], ss.at[0], rs.at[0], pv, pf).start()
        return c

    lax.fori_loop(1, n, scatter, 0)

    def coarse(t, c):
        r = 2 * t
        o = dot(ck[...], pair(psh, r, taps))
        cor[r] = o[:, :half]
        cor[r + 1] = o[:, half:]
        return c

    lax.fori_loop(0, rows // 2, coarse, 0, unroll=2)
    co[...] = jnp.transpose(cor[...], (1, 0, 2)).astype(BF16).reshape(co.shape)
    spot = out.at[:, pl.ds(pl.multiple_of(f * rows, rows), rows)]
    mine = pltpu.make_async_copy(co.at[f], spot, ls.at[1])
    mine.start()
    copies = []
    for d in range(1, F):
        far = lax.rem(f + d, F)
        copies.append(remote(co.at[far], spot, os.at[d], orr.at[d], v, far))
        copies[-1].start()
    pltpu.make_async_copy(slots, slots, rs.at[0]).wait()
    here = pl.ds(pl.multiple_of(me * chunk, chunk), chunk)
    red[...] = (g[here].astype(F32) + jnp.sum(slots[...].astype(F32), axis=0)).astype(red.dtype)
    total[here] = red[...]

    def gather(d, c):
        _, pv, pf = peer_of(d)
        remote(red, total.at[here], ss.at[1], rs.at[1], pv, pf).start()
        return c

    lax.fori_loop(1, n, gather, 0)
    mine.wait()
    for c in copies:
        c.wait()
    pltpu.make_async_copy(slots, slots, ss.at[0]).wait()
    pltpu.make_async_copy(slots, slots, rs.at[1]).wait()
    pltpu.make_async_copy(slots, slots, ss.at[1]).wait()
    for at, (s, a, b) in enumerate(span):
        block = total[at * chans : (at + 1) * chans, :].astype(F32)
        gc_out[a, b, s] = block[:, :outs]
        gf_out[a, b, s] = block[:, outs : outs + chans]


def local(V, F, volume, fine_kernel, coarse_kernel, coarse_cot):
    chans, planes, frows, cols = volume.shape
    filters, _, allrows, half = coarse_cot.shape
    rows = allrows // F
    outs = filters * F
    n = V * F
    taps = 27 * chans
    chunk = 16 * (-(-taps // (16 * n)))
    vmem = pl.BlockSpec(memory_space=pltpu.VMEM)
    dma = pltpu.SemaphoreType.DMA

    def call(body, ins, outputs, scratch, ident=None):
        extra = {} if ident is None else dict(collective_id=ident, has_side_effects=True)
        return pl.pallas_call(
            body,
            out_shape=[jax.ShapeDtypeStruct(s, t) for s, t in outputs],
            in_specs=[pl.BlockSpec(memory_space=pltpu.HBM)] * ins,
            out_specs=[vmem] * len(outputs),
            scratch_shapes=scratch,
            compiler_params=pltpu.CompilerParams(vmem_limit_bytes=56 * 2**20, **extra),
        )

    fk = fine_kernel.transpose(2, 3, 4, 0, 1)
    kk = coarse_kernel.transpose(2, 3, 4, 1, 0)
    out, gc, gf = call(
        functools.partial(whole_kernel, V, F),
        4,
        [
            ((filters, allrows, half), BF16),
            ((3, 3, 3, chans, outs), F32),
            ((3, 3, 3, chans, chans), F32),
        ],
        [
            pltpu.VMEM(volume.shape, BF16),
            pltpu.VMEM(coarse_cot.shape, BF16),
            pltpu.VMEM(fk.shape, BF16),
            pltpu.VMEM(kk.shape, BF16),
            pltpu.VMEM((planes, frows, chans, cols), BF16),
            pltpu.VMEM((allrows + 2, filters, half), BF16),
            pltpu.VMEM((rows, outs, half), F32),
            pltpu.VMEM((4 * chans, 48 * chans), BF16),
            pltpu.VMEM((outs, taps), BF16),
            pltpu.VMEM((3 * chans, 9 * outs), BF16),
            pltpu.VMEM((n * chunk, 128), BF16),
            pltpu.VMEM((3, rows, chans, half), F32),
            pltpu.VMEM((2, rows, chans, half), F32),
            pltpu.VMEM((planes + 2, frows + 2, chans, cols), BF16),
            pltpu.VMEM((F, rows + 2, filters, half), BF16),
            pltpu.VMEM((3, planes + 2, frows + 2, chans, cols), BF16),
            pltpu.VMEM((rows, 4 * chans, cols), BF16),
            pltpu.VMEM((3, rows + 2, chans, half), BF16),
            pltpu.VMEM((3, 3, rows + 2, chans, half), BF16),
            pltpu.VMEM((3, rows + 2, outs, half), BF16),
            pltpu.VMEM((taps, outs), F32),
            pltpu.VMEM((48 * chans, 4 * chans), F32),
            pltpu.VMEM((F, filters, rows, half), BF16),
            pltpu.VMEM((n * chunk, 128), BF16),
            pltpu.VMEM((n - 1, chunk, 128), BF16),
            pltpu.VMEM((chunk, 128), BF16),
        ]
        + [dma((k,)) for k in (8, 8, F, F, 2, 2, 8, 8, F, F, 2, 2, 2, 4)],
        0,
    )(volume, coarse_cot, fk, kk)
    coarse_out = out[:, None]
    return coarse_out, gf.transpose(4, 3, 0, 1, 2), gc.transpose(4, 3, 0, 1, 2)


def solution(mesh):
    from jax.sharding import PartitionSpec as P

    in_specs = (P(None, "vox", "fil", None), P(), P(), P("fil", "vox", None, None))
    out_specs = (P("fil", "vox", None, None), P(), P())
    body = functools.partial(local, mesh.shape["vox"], mesh.shape["fil"])
    return jax.shard_map(body, mesh=mesh, in_specs=in_specs, out_specs=out_specs, check_vma=False)
```
